32 devices in a mesh: slab: 8 (over y, x, core), coil: 4 (over z).
Axes of the slice: x: 2, y: 2, z: 4, core: 2. Of those that a mesh axis runs over, the one named last changes fastest.
Arguments:
- samples: bfloat16 [8, 65536, 128], P('coil', 'slab'), may hold values from -6 to 6
- sample_pos: bfloat16 [65536, 64], P('slab'), may hold values from 0 to 64
- block_count: int32 [65536], P('slab'), may hold values from 16 to 64
- grid_block: int32 [65536], P('slab'), may hold values from 0 to 32767
- block_slab: int32 [65536, 1], P('slab'), may hold values from 0 to 7, as said below
- sensitivity: bfloat16 [8, 256, 16, 512], P(None, 'slab', 'coil'), may hold values from -3 to 3
Outputs:
- image: float32 [256, 16, 512], P('slab', 'coil')
The draws below stay inside these ranges and needn't reach their ends.
Inputs may be any that keep to these rules, and one draw needn't show every extreme that they name: `block_slab`: within the rows of one device no slab is named more than 2560 times; one slab, the same for every device, is named exactly 2560 times by every device.
All inputs are finite; a program needn't handle non-finite values.
Results may differ from the reference program's by a relative error of at most 0.02.
The reference program's roundings to bfloat16 on the way count: a program that leaves them out, or rounds other values in their place, can miss the bound.
Values may be sent and summed in bfloat16 or wider, within the bound.
A program may use at most 128 MiB of HBM per device.

```python
import math
import jax
import jax.numpy as jnp
from jax import lax

COILS = 8
KX = 256
KY = 256
Z = 256
BLOCK_LEN = 64
XW = 16
BLK_DEV = 8192
ZP = 32
BLOCKS = 65536
CAP = 2560
NGB = 32768


def draw_block_slab(key, part):
    slab_total = BLOCKS // BLK_DEV
    remaining = BLK_DEV - CAP
    key_busy, key_share, key_order = jax.random.split(key, 3)
    busiest = jax.random.randint(key_busy, (), 0, slab_total)
    row_index = jnp.arange(BLK_DEV, dtype=jnp.int32)
    beyond = jnp.maximum(row_index - CAP, 0)

    def one_device(share_key, order_key):
        shares = jax.random.randint(share_key, (slab_total - 1,), 1, 3)
        bounds = remaining * jnp.cumsum(shares) // jnp.sum(shares)
        other_slab = 1 + jnp.sum((bounds[None, :] <= beyond[:, None]).astype(jnp.int32), axis=1)
        offset_row = jnp.where(row_index < CAP, 0, other_slab)
        slab_of = (busiest + offset_row) % slab_total
        return slab_of[jax.random.permutation(order_key, BLK_DEV)]
    drawn = jax.vmap(one_device)(jax.random.split(key_share, slab_total), jax.random.split(key_order, slab_total))
    return drawn.reshape(BLOCKS, 1).astype(jnp.int32)


def set_ends(values, key, smallest, largest):
    spot = [jax.random.randint(jax.random.fold_in(key, axis), (), 0, length) for axis, length in enumerate(values.shape)]
    widest = values.shape.index(max(values.shape))
    beside = spot[:widest] + [(spot[widest] + 1) % values.shape[widest]] + spot[widest + 1:]
    return values.at[tuple(spot)].set(smallest).at[tuple(beside)].set(largest)


def level_of(key, dims, cuts, low, high):
    def one(dim, blocks):
        steps = jax.random.uniform(jax.random.fold_in(jax.random.fold_in(key, 6), dim), (blocks,), jnp.float32, low / len(cuts), high / len(cuts))
        return jnp.repeat(jnp.exp(steps), dims[dim] // blocks).reshape((-1,) + (1,) * (len(dims) - dim - 1))

    loudness = one(*cuts[0])
    for cut in cuts[1:]:
        loudness = loudness * one(*cut)
    return loudness


def centred(key, dims, deviation, most, cuts=(), kind=jnp.bfloat16):
    values = deviation * jax.random.normal(key, dims, jnp.float32)
    if cuts:
        values = values * level_of(key, dims, cuts, -0.22, 0.18)
    return jnp.clip(values, -most, most).astype(kind)


def setup_inputs(seed: int = 0) -> dict:
    keys = jax.random.split(jax.random.key(seed), 7)
    return {
        "samples": centred(keys[0], (COILS, BLOCKS, 2 * BLOCK_LEN), 1.0, 6.0, ((0, 4), (1, 8))),
        "sample_pos": jnp.clip(64.0 * jax.random.uniform(keys[1], (BLOCKS, BLOCK_LEN), jnp.float32) ** level_of(keys[1], (BLOCKS, BLOCK_LEN), ((0, 8),), -0.2, 0.2), 0.0, 64.0).astype(jnp.bfloat16),
        "block_count": set_ends(jax.random.randint(keys[2], (BLOCKS,), 16, BLOCK_LEN + 1), jax.random.fold_in(keys[2], 1), 16, BLOCK_LEN).astype(jnp.int32),
        "grid_block": set_ends(jax.random.randint(keys[3], (BLOCKS,), 0, NGB), jax.random.fold_in(keys[3], 1), 0, NGB - 1).astype(jnp.int32),
        "block_slab": draw_block_slab(jax.random.fold_in(keys[6], 71), 0),
        "sensitivity": centred(keys[5], (COILS, Z, XW, 2 * KY), 0.5, 3.0, ((1, 8), (2, 4))),
    }


kernel_half = 2.5

def block_weights(positions, counts):
    cell_mid = jnp.arange(positions.shape[-1], dtype=jnp.int32).astype(jnp.float32) + 0.5
    offset = (positions.astype(jnp.float32)[..., :, None] - cell_mid) / kernel_half
    bump = jnp.maximum(1.0 - offset * offset, 0.0)
    live = jnp.arange(positions.shape[-1], dtype=jnp.int32)[:, None] < counts[..., None, None]
    return jnp.where(live, bump * bump, 0.0).astype(jnp.bfloat16)

def twiddle(first, second, length):
    phase = (first * second % length).astype(jnp.float32) * (2.0 * math.pi / length)
    scale = 1.0 / math.sqrt(length)
    return (jnp.cos(phase) * scale, jnp.sin(phase) * scale)

def choose(part_in, part_out, cosine, sine):
    upper = jnp.where(part_out == 0, cosine, sine)
    lower = jnp.where(part_out == 0, -sine, cosine)
    return jnp.where(part_in == 0, upper, lower).astype(jnp.bfloat16)

def across_table(kx_len, rows_out):
    index_in = jnp.arange(2 * kx_len, dtype=jnp.int32)
    segment = index_in // 128
    part_in = index_in // 64 % 2
    cell_at = segment * 64 + index_in % 64
    index_out = jnp.arange(2 * rows_out, dtype=jnp.int32)
    part_out = index_out // rows_out
    row_at = (kx_len - rows_out) // 2 + index_out % rows_out
    cosine, sine = twiddle(cell_at[:, None], row_at[None, :], kx_len)
    return choose(part_in[:, None], part_out[None, :], cosine, sine)

def square_table(length):
    index_in = jnp.arange(2 * length, dtype=jnp.int32)
    index_out = jnp.arange(2 * length, dtype=jnp.int32)
    cosine, sine = twiddle((index_in // 2)[:, None], (index_out % length)[None, :], length)
    return choose((index_in % 2)[:, None], (index_out // length)[None, :], cosine, sine)

def depth_table(positions, freqs, length):
    cosine, sine = twiddle(positions[:, None], freqs[None, :], length)
    upper = jnp.stack([cosine, -sine], axis=-1)
    lower = jnp.stack([sine, cosine], axis=-1)
    return jnp.stack([upper, lower], axis=1).astype(jnp.bfloat16)

def conj_term(coil_map, coil_image, half):
    map_re = coil_map[..., :half].astype(jnp.float32)
    map_im = coil_map[..., half:].astype(jnp.float32)
    img_re = coil_image[..., :half].astype(jnp.float32)
    img_im = coil_image[..., half:].astype(jnp.float32)
    return jnp.concatenate([map_re * img_re + map_im * img_im, map_re * img_im - map_im * img_re], axis=-1)

def reference(samples, sample_pos, block_count, grid_block, block_slab, sensitivity):
    seg_count = KX // 64
    target = (block_slab[:, 0] * (ZP * KY * seg_count) + grid_block).astype(jnp.int32)
    group_len = math.gcd(BLOCKS, 4096)
    group_count = BLOCKS // group_len

    def one_group(pieces):
        values, positions, counts = pieces
        weights = lax.optimization_barrier(block_weights(positions, counts)).astype(jnp.float32)
        shaped = values.astype(jnp.float32).reshape(COILS, group_len, 2, 64)
        result = jnp.einsum('mij,cmpi->cmpj', weights, shaped, precision=lax.Precision.HIGHEST)
        return result.reshape(COILS, group_len, 128).astype(jnp.bfloat16)
    grouped = (jnp.transpose(samples.reshape(COILS, group_count, group_len, 128), (1, 0, 2, 3)), sample_pos.reshape(group_count, group_len, 64), block_count.reshape(group_count, group_len))
    gridded = jnp.transpose(lax.map(one_group, grouped), (1, 0, 2, 3)).reshape(COILS, BLOCKS, 128)
    across = across_table(KX, XW)
    y_table = square_table(KY).reshape(KY, 2, 2 * KY).astype(jnp.float32)
    every_z = jnp.arange(Z, dtype=jnp.int32)
    depth_tab = depth_table(every_z, every_z, Z).astype(jnp.float32)

    def one_coil(running, pieces):
        cell_rows, coil_map = pieces
        cell_wide = lax.optimization_barrier(cell_rows).astype(jnp.float32)
        kspace = jnp.zeros((Z * KY * seg_count, 128), jnp.float32).at[target].add(cell_wide).astype(jnp.bfloat16)
        x_rows = jnp.dot(kspace.reshape(Z * KY, 2 * KX), across, preferred_element_type=jnp.float32).astype(jnp.bfloat16)
        x_rows = lax.optimization_barrier(x_rows).astype(jnp.float32).reshape(Z, KY, 2, XW)
        y_planes = jnp.einsum('zkqx,kqn->zxn', x_rows, y_table, precision=lax.Precision.HIGHEST).astype(jnp.bfloat16)
        y_planes = lax.optimization_barrier(y_planes).astype(jnp.float32).reshape(Z, XW, 2, KY)
        coil_image = jnp.einsum('zpkq,kxqy->zxpy', depth_tab, y_planes, precision=lax.Precision.HIGHEST)
        coil_image = coil_image.reshape(Z, XW, 2 * KY).astype(jnp.bfloat16)
        return (running + conj_term(coil_map, coil_image, KY), None)
    start_sum = jnp.zeros((Z, XW, 2 * KY), jnp.float32)
    image, _ = lax.scan(one_coil, start_sum, (gridded, sensitivity))
    return image
```

```python
import functools
import math

import jax
import jax.numpy as jnp
from jax import lax
from jax.experimental import pallas as pl
from jax.experimental.pallas import tpu as pltpu
from jax.sharding import PartitionSpec as P

KX = 256
CELLS = 64
NT = (((1,), (1,)), ((), ()))


def twiddle(first, second, length):
    phase = (first * second % length).astype(jnp.float32) * (2.0 * math.pi / length)
    scale = 1.0 / math.sqrt(length)
    return (jnp.cos(phase) * scale, jnp.sin(phase) * scale)


def ints(count):
    return jnp.arange(count, dtype=jnp.int32)


def across_stack(rows_out, stacked):
    x0 = (KX - rows_out) // 2
    cosine, sine = twiddle(x0 + ints(rows_out)[:, None], ints(CELLS)[None, :], KX)
    table = jnp.concatenate([cosine, sine], axis=0)
    eye = jnp.eye(stacked, dtype=jnp.float32)
    full = eye[:, None, :, None] * table[None, :, None, :]
    return full.reshape(stacked * 2 * rows_out, stacked * CELLS).astype(jnp.bfloat16)


def right_table(length):
    cosine, sine = twiddle(ints(length)[:, None], ints(length)[None, :], length)
    upper = jnp.concatenate([cosine, sine], axis=1)
    lower = jnp.concatenate([-sine, cosine], axis=1)
    return jnp.concatenate([upper, lower], axis=0).astype(jnp.bfloat16)


def left_table(length):
    cosine, sine = twiddle(ints(length)[:, None], ints(length)[None, :], length)
    upper = jnp.concatenate([cosine, -sine], axis=1)
    lower = jnp.concatenate([sine, cosine], axis=1)
    return jnp.concatenate([upper, lower], axis=0).astype(jnp.bfloat16)


def grid_kernel(stacked, coils, rows_out, pos_ref, val_ref, seg_ref, tab_ref, out_ref, wide):
    lanes = pos_ref.shape[1]
    wide[...] = val_ref[...].astype(jnp.float32)
    mid = (lax.broadcasted_iota(jnp.int32, (CELLS, lanes), 0).astype(jnp.float32) + 0.5) * 0.4
    table = tab_ref[...]

    def step(at, sums):
        parts = []
        for k in range(stacked):
            offset = pos_ref[pl.ds(at * stacked + k, 1), :] - mid
            bump = jnp.maximum(1.0 - offset * offset, 0.0)
            parts.append((bump * bump).astype(jnp.bfloat16))
        moved = jnp.dot(
            table, jnp.concatenate(parts, axis=0), preferred_element_type=jnp.float32
        )
        sums = list(sums)
        for k in range(stacked):
            base = k * 2 * rows_out
            cosine = moved[base : base + rows_out]
            sine = moved[base + rows_out : base + 2 * rows_out]
            for c in range(coils):
                re = wide[c, pl.ds(at * stacked + k, 1), :]
                im = wide[c, pl.ds(CELLS + at * stacked + k, 1), :]
                sums[2 * c] = sums[2 * c] + (re * cosine - im * sine)
                sums[2 * c + 1] = sums[2 * c + 1] + (re * sine + im * cosine)
        return tuple(sums)

    zero = jnp.zeros((rows_out, lanes), jnp.float32)
    sums = lax.fori_loop(0, CELLS // stacked, step, (zero,) * (2 * coils))
    x_at = lax.broadcasted_iota(jnp.int32, (rows_out, lanes), 0) + (KX - rows_out) // 2
    turn = (x_at * seg_ref[...]) & 3
    for c in range(coils):
        re, im = sums[2 * c], sums[2 * c + 1]
        new_re = jnp.where((turn & 1) == 0, re, -im)
        new_im = jnp.where((turn & 1) == 0, im, re)
        sign = jnp.where(turn >= 2, -1.0, 1.0)
        out_ref[2 * c] = (new_re * sign).astype(jnp.bfloat16)
        out_ref[2 * c + 1] = (new_im * sign).astype(jnp.bfloat16)


def sort_kernel(vals_ref, rank_ref, out_ref):
    group = vals_ref.shape[1]
    tile = min(256, group)

    @pl.loop(0, group // tile)
    def _(at):
        start = pl.multiple_of(at * tile, tile)
        slot = lax.broadcasted_iota(jnp.int32, (tile, group), 0) + start
        hot = jnp.where(slot == rank_ref[...], 1.0, 0.0).astype(jnp.bfloat16)
        moved = lax.dot_general(vals_ref[...], hot, NT, preferred_element_type=jnp.float32)
        out_ref[:, pl.ds(start, tile)] = moved.astype(jnp.bfloat16)


def add_kernel(
    chunk, span, lo_ref, hi_ref, vals_ref, kz_ref, ky_ref, ytab_ref, ztab_ref, out_ref, total
):
    step = pl.program_id(0)
    rows = vals_ref.shape[1]
    width = vals_ref.shape[2]
    depth, freq = total.shape[1], total.shape[2]

    @pl.when(step == 0)
    def _():
        total[...] = jnp.zeros_like(total)

    for part in range(width // chunk):
        cut = slice(part * chunk, (part + 1) * chunk)
        spot = lax.broadcasted_iota(jnp.int32, (freq, chunk), 0)
        hot = jnp.where(spot == ky_ref[0, :, cut], 1.0, 0.0).astype(jnp.bfloat16)
        plane = lax.broadcasted_iota(jnp.int32, (span, chunk), 0)
        kz = kz_ref[0, :, cut]
        vals = [vals_ref[0, v : v + 1, cut].astype(jnp.float32) for v in range(rows)]
        at_chunk = step * (width // chunk) + part

        def one(at, carry):
            start = pl.multiple_of(at * span, span)
            mine = plane == (kz - start)
            left = jnp.concatenate(
                [jnp.where(mine, vals[v], 0.0).astype(jnp.bfloat16) for v in range(rows)], axis=0
            )
            moved = lax.dot_general(left, hot, NT, preferred_element_type=jnp.float32)
            for v in range(rows):
                total[v, pl.ds(start, span), :] += moved[v * span : (v + 1) * span]
            return carry

        lax.fori_loop(lo_ref[at_chunk], hi_ref[at_chunk], one, 0)

    @pl.when(step == pl.num_programs(0) - 1)
    def _():
        pairs = rows // 2
        for pair in range(pairs):
            both = jnp.concatenate([total[2 * pair], total[2 * pair + 1]], axis=1)
            planes = jnp.dot(
                both.astype(jnp.bfloat16), ytab_ref[...], preferred_element_type=jnp.float32
            ).astype(jnp.bfloat16)
            planes = jnp.concatenate([planes[:, :freq], planes[:, freq:]], axis=0)
            image = jnp.dot(ztab_ref[...], planes, preferred_element_type=jnp.float32)
            out_ref[pair, :, :freq] = image[:depth].astype(jnp.bfloat16)
            out_ref[pair, :, freq:] = image[depth:].astype(jnp.bfloat16)


def whole(memory=pltpu.VMEM):
    return pl.BlockSpec(memory_space=memory)


def per_device(samples, sample_pos, block_count, grid_block, block_slab, sensitivity):
    slab_total = lax.axis_size("slab")
    coil_total = lax.axis_size("coil")
    coils = samples.shape[0]
    blocks = samples.shape[1]
    planes = sensitivity.shape[1]
    rows_out = sensitivity.shape[2] * coil_total
    depth = planes * slab_total
    freq = sensitivity.shape[3] // 2
    x_here = rows_out // slab_total
    segments = KX // CELLS

    live = ints(CELLS)[:, None] < block_count[None, :]
    pos = jnp.where(live, sample_pos.T.astype(jnp.float32), 1.0e4) * 0.4
    vals = jnp.swapaxes(samples, 1, 2)
    seg = (grid_block % segments)[None, :]
    kz = block_slab[:, 0] * planes + grid_block // (segments * freq)
    ky = grid_block // segments % freq

    stacked = 4
    tile = math.gcd(blocks, 256)
    table = across_stack(rows_out, stacked)
    spread = pl.pallas_call(
        functools.partial(grid_kernel, stacked, coils, rows_out),
        grid=(blocks // tile,),
        in_specs=[
            pl.BlockSpec((CELLS, tile), lambda b: (0, b)),
            pl.BlockSpec((coils, 2 * CELLS, tile), lambda b: (0, 0, b)),
            pl.BlockSpec((1, tile), lambda b: (0, b)),
            pl.BlockSpec(table.shape, lambda b: (0, 0)),
        ],
        out_specs=pl.BlockSpec((2 * coils, rows_out, tile), lambda b: (0, 0, b)),
        out_shape=jax.ShapeDtypeStruct((2 * coils, rows_out, blocks), jnp.bfloat16),
        scratch_shapes=[pltpu.VMEM((coils, 2 * CELLS, tile), jnp.float32)],
        name="grid_x",
    )(pos, vals, seg, table)

    group = math.gcd(blocks, 2048)
    groups = blocks // group
    key = (kz * group + ints(blocks) % group).reshape(groups, group)
    rank = jnp.sum((key[:, :, None] < key[:, None, :]).astype(jnp.int32), axis=1)
    rank = rank.reshape(1, blocks)
    lines = spread.reshape(coils, 2, slab_total, x_here, blocks)
    lines = jnp.transpose(lines, (2, 0, 3, 1, 4)).reshape(2 * coils * rows_out, blocks)
    spots = jnp.stack([kz, ky]).astype(jnp.bfloat16)
    lines = jnp.concatenate([lines, jnp.pad(spots, ((0, 14), (0, 0)))], axis=0)
    ordered = pl.pallas_call(
        sort_kernel,
        grid=(groups,),
        in_specs=[
            pl.BlockSpec((lines.shape[0], group), lambda b: (0, b)),
            pl.BlockSpec((1, group), lambda b: (0, b)),
        ],
        out_specs=pl.BlockSpec((lines.shape[0], group), lambda b: (0, b)),
        out_shape=jax.ShapeDtypeStruct(lines.shape, jnp.bfloat16),
        name="order_kz",
    )(lines, rank)
    count = 2 * coils * rows_out
    each = 2 * coils * x_here
    sent = lax.all_to_all(
        ordered[:count].reshape(slab_total, each, blocks), "slab", 0, 0, tiled=True
    )
    spots = lax.all_gather(ordered[count : count + 2], "slab", axis=0)
    spots = spots.astype(jnp.int32)
    kz_all = spots[:, 0:1]
    ky_all = spots[:, 1:2]

    chunk = math.gcd(blocks, 256)
    span = math.gcd(depth, 32)
    width = math.gcd(blocks, 1024)
    per_row = blocks // width
    by_chunk = kz_all.reshape(slab_total * blocks // chunk, chunk)
    low = jnp.min(by_chunk, axis=1) // span
    high = jnp.max(by_chunk, axis=1) // span + 1
    ytab, ztab = right_table(freq), left_table(depth)
    pairs = each // 2
    imaged = pl.pallas_call(
        functools.partial(add_kernel, chunk, span),
        grid_spec=pltpu.PrefetchScalarGridSpec(
            num_scalar_prefetch=2,
            grid=(slab_total * per_row,),
            in_specs=[
                pl.BlockSpec((1, each, width), lambda i, a, b: (i // per_row, 0, i % per_row)),
                pl.BlockSpec((1, 1, width), lambda i, a, b: (i // per_row, 0, i % per_row)),
                pl.BlockSpec((1, 1, width), lambda i, a, b: (i // per_row, 0, i % per_row)),
                pl.BlockSpec(ytab.shape, lambda i, a, b: (0, 0)),
                pl.BlockSpec(ztab.shape, lambda i, a, b: (0, 0)),
            ],
            out_specs=pl.BlockSpec((pairs, depth, 2 * freq), lambda i, a, b: (0, 0, 0)),
            scratch_shapes=[pltpu.VMEM((each, depth, freq), jnp.float32)],
        ),
        out_shape=jax.ShapeDtypeStruct((pairs, depth, 2 * freq), jnp.bfloat16),
        name="add_yz",
    )(low, high, sent, kz_all, ky_all, ytab, ztab)

    split = imaged.reshape(pairs, slab_total, planes, 2 * freq)
    split = lax.all_to_all(jnp.swapaxes(split, 0, 1), "slab", 0, 0, tiled=True)
    split = split.reshape(slab_total, coils, x_here, planes, 2 * freq)
    split = jnp.transpose(split, (0, 2, 1, 3, 4)).reshape(
        coil_total, rows_out // coil_total, coils, planes, 2 * freq
    )
    split = lax.all_to_all(split, "coil", 0, 0, tiled=True)
    mine = jnp.transpose(split, (0, 2, 3, 1, 4)).reshape(sensitivity.shape).astype(jnp.float32)
    maps = sensitivity.astype(jnp.float32)
    map_re, map_im = maps[..., :freq], maps[..., freq:]
    img_re, img_im = mine[..., :freq], mine[..., freq:]
    real_part = jnp.sum(map_re * img_re + map_im * img_im, axis=0)
    imag_part = jnp.sum(map_re * img_im - map_im * img_re, axis=0)
    return jnp.concatenate([real_part, imag_part], axis=-1)


def solution(mesh):
    return jax.shard_map(
        per_device,
        mesh=mesh,
        in_specs=(
            P("coil", "slab", None),
            P("slab", None),
            P("slab"),
            P("slab"),
            P("slab", None),
            P(None, "slab", "coil", None),
        ),
        out_specs=P("slab", "coil", None),
        check_vma=False,
    )
```

```python
import functools
import math

import jax
import jax.numpy as jnp
from jax import lax
from jax.experimental import pallas as pl
from jax.experimental.pallas import tpu as pltpu
from jax.sharding import PartitionSpec as P

KX = 256
CELLS = 64
NT = (((1,), (1,)), ((), ()))


def twiddle(first, second, length):
    phase = (first * second % length).astype(jnp.float32) * (2.0 * math.pi / length)
    scale = 1.0 / math.sqrt(length)
    return (jnp.cos(phase) * scale, jnp.sin(phase) * scale)


def ints(count):
    return jnp.arange(count, dtype=jnp.int32)


def across_table(rows_out):
    x0 = (KX - rows_out) // 2
    cosine, sine = twiddle(x0 + ints(rows_out)[:, None], ints(CELLS)[None, :], KX)
    return jnp.concatenate([cosine, sine], axis=0).astype(jnp.bfloat16)


def right_table(length):
    cosine, sine = twiddle(ints(length)[:, None], ints(length)[None, :], length)
    upper = jnp.concatenate([cosine, sine], axis=1)
    lower = jnp.concatenate([-sine, cosine], axis=1)
    return jnp.concatenate([upper, lower], axis=0).astype(jnp.bfloat16)


def left_table(length):
    cosine, sine = twiddle(ints(length)[:, None], ints(length)[None, :], length)
    upper = jnp.concatenate([cosine, -sine], axis=1)
    lower = jnp.concatenate([sine, cosine], axis=1)
    return jnp.concatenate([upper, lower], axis=0).astype(jnp.bfloat16)


def grid_kernel(coils, rows_out, pos_ref, val_ref, seg_ref, tab_ref, out_ref, wide, where):
    lanes = wide.shape[2]
    mid = (lax.broadcasted_iota(jnp.int32, (CELLS, lanes), 0).astype(jnp.float32) + 0.5) * 0.4
    x_at = lax.broadcasted_iota(jnp.int32, (rows_out, lanes), 0) + (KX - rows_out) // 2

    @pl.loop(0, pos_ref.shape[1] // lanes)
    def _(at):
        cut = pl.ds(pl.multiple_of(at * lanes, lanes), lanes)
        wide[...] = val_ref[:, :, cut].astype(jnp.float32)
        where[...] = pos_ref[:, cut]

        def step(i, sums):
            offset = where[pl.ds(i, 1), :] - mid
            bump = jnp.maximum(1.0 - offset * offset, 0.0)
            weight = (bump * bump).astype(jnp.bfloat16).astype(jnp.float32)
            return tuple(
                sums[n] + weight * wide[n // 2, pl.ds(n % 2 * CELLS + i, 1), :]
                for n in range(2 * coils)
            )

        zero = jnp.zeros((CELLS, lanes), jnp.float32)
        sums = lax.fori_loop(0, CELLS, step, (zero,) * (2 * coils), unroll=4)
        turn = (x_at * seg_ref[:, cut]) & 3
        sign = jnp.where(turn >= 2, -1.0, 1.0)
        cells = jnp.concatenate([part.astype(jnp.bfloat16) for part in sums], axis=1)
        moved = jnp.dot(tab_ref[...], cells, preferred_element_type=jnp.float32)
        for c in range(coils):
            of_re = moved[:, 2 * c * lanes : (2 * c + 1) * lanes]
            of_im = moved[:, (2 * c + 1) * lanes : (2 * c + 2) * lanes]
            re = of_re[:rows_out] - of_im[rows_out:]
            im = of_re[rows_out:] + of_im[:rows_out]
            new_re = jnp.where((turn & 1) == 0, re, -im)
            new_im = jnp.where((turn & 1) == 0, im, re)
            out_ref[2 * c, :, cut] = (new_re * sign).astype(jnp.bfloat16)
            out_ref[2 * c + 1, :, cut] = (new_im * sign).astype(jnp.bfloat16)


def sort_kernel(vals_ref, rank_ref, out_ref):
    group = vals_ref.shape[1]
    tile = min(256, group)

    @pl.loop(0, group // tile)
    def _(at):
        start = pl.multiple_of(at * tile, tile)
        slot = lax.broadcasted_iota(jnp.int32, (tile, group), 0) + start
        hot = jnp.where(slot == rank_ref[...], 1.0, 0.0).astype(jnp.bfloat16)
        moved = lax.dot_general(vals_ref[...], hot, NT, preferred_element_type=jnp.float32)
        out_ref[:, pl.ds(start, tile)] = moved.astype(jnp.bfloat16)


def add_kernel(
    chunk, span, lo_ref, more_ref, vals_ref, kz_ref, ky_ref, ytab_ref, ztab_ref, out_ref, total
):
    step = pl.program_id(0)
    rows = vals_ref.shape[1]
    width = vals_ref.shape[2]
    depth, freq = out_ref.shape[1], total.shape[2]
    parts = width // chunk
    spot = lax.broadcasted_iota(jnp.int32, (freq, chunk), 0)
    plane = lax.broadcasted_iota(jnp.int32, (span, chunk), 0)

    @pl.when(step == 0)
    def _():
        total[...] = jnp.zeros_like(total)

    def add(part, start):
        cut = slice(part * chunk, (part + 1) * chunk)
        hot = jnp.where(spot == ky_ref[0, :, cut], 1.0, 0.0).astype(jnp.bfloat16)
        mine = jnp.where(plane == (kz_ref[0, :, cut] - start), 1.0, 0.0).astype(jnp.bfloat16)
        left = []
        for v in range(rows):
            row = vals_ref[0, v : v + 1, cut].astype(jnp.float32)
            row = jnp.broadcast_to(row, (16, chunk)).astype(jnp.bfloat16)
            left.append(mine * jnp.concatenate([row] * (span // 16), axis=0))
        left = jnp.concatenate(left, axis=0)
        moved = lax.dot_general(left, hot, NT, preferred_element_type=jnp.float32)
        for v in range(rows):
            total[v, pl.ds(start, span), :] += moved[v * span : (v + 1) * span]

    for part in range(parts):
        add(part, pl.multiple_of(lo_ref[step * parts + part], 8))

    for part in range(parts):
        first = lo_ref[step * parts + part]

        def again(at, carry):
            add(part, pl.multiple_of(first + at * span, 8))
            return carry

        lax.fori_loop(1, more_ref[step * parts + part], again, 0)

    @pl.when(step == pl.num_programs(0) - 1)
    def _():
        pairs = rows // 2
        for pair in range(pairs):
            both = jnp.concatenate(
                [total[2 * pair, :depth, :], total[2 * pair + 1, :depth, :]], axis=1
            )
            planes = jnp.dot(
                both.astype(jnp.bfloat16), ytab_ref[...], preferred_element_type=jnp.float32
            ).astype(jnp.bfloat16)
            planes = jnp.concatenate([planes[:, :freq], planes[:, freq:]], axis=0)
            image = jnp.dot(ztab_ref[...], planes, preferred_element_type=jnp.float32)
            out_ref[pair, :, :freq] = image[:depth].astype(jnp.bfloat16)
            out_ref[pair, :, freq:] = image[depth:].astype(jnp.bfloat16)


def whole(memory=pltpu.VMEM):
    return pl.BlockSpec(memory_space=memory)


def per_device(samples, sample_pos, block_count, grid_block, block_slab, sensitivity):
    slab_total = lax.axis_size("slab")
    coil_total = lax.axis_size("coil")
    coils = samples.shape[0]
    blocks = samples.shape[1]
    planes = sensitivity.shape[1]
    rows_out = sensitivity.shape[2] * coil_total
    depth = planes * slab_total
    freq = sensitivity.shape[3] // 2
    x_here = rows_out // slab_total
    segments = KX // CELLS

    live = ints(CELLS)[:, None] < block_count[None, :]
    pos = jnp.where(live, sample_pos.T.astype(jnp.float32), 1.0e4) * 0.4
    vals = jnp.swapaxes(samples, 1, 2)
    seg = (grid_block % segments)[None, :]
    kz = block_slab[:, 0] * planes + grid_block // (segments * freq)
    ky = grid_block // segments % freq

    tile = math.gcd(blocks, 1024)
    table = across_table(rows_out)
    spread = pl.pallas_call(
        functools.partial(grid_kernel, coils, rows_out),
        grid=(blocks // tile,),
        in_specs=[
            pl.BlockSpec((CELLS, tile), lambda b: (0, b)),
            pl.BlockSpec((coils, 2 * CELLS, tile), lambda b: (0, 0, b)),
            pl.BlockSpec((1, tile), lambda b: (0, b)),
            pl.BlockSpec(table.shape, lambda b: (0, 0)),
        ],
        out_specs=pl.BlockSpec((2 * coils, rows_out, tile), lambda b: (0, 0, b)),
        out_shape=jax.ShapeDtypeStruct((2 * coils, rows_out, blocks), jnp.bfloat16),
        scratch_shapes=[
            pltpu.VMEM((coils, 2 * CELLS, math.gcd(tile, 128)), jnp.float32),
            pltpu.VMEM((CELLS, math.gcd(tile, 128)), jnp.float32),
        ],
        name="grid_x",
    )(pos, vals, seg, table)

    group = math.gcd(blocks, 2048)
    groups = blocks // group
    key = (kz * group + ints(blocks) % group).reshape(groups, group)
    rank = jnp.sum((key[:, :, None] < key[:, None, :]).astype(jnp.int32), axis=1)
    rank = rank.reshape(1, blocks)
    lines = spread.reshape(coils, 2, slab_total, x_here, blocks)
    lines = jnp.transpose(lines, (2, 0, 3, 1, 4)).reshape(2 * coils * rows_out, blocks)
    spots = jnp.stack([kz, ky]).astype(jnp.bfloat16)
    lines = jnp.concatenate([lines, jnp.pad(spots, ((0, 14), (0, 0)))], axis=0)
    ordered = pl.pallas_call(
        sort_kernel,
        grid=(groups,),
        in_specs=[
            pl.BlockSpec((lines.shape[0], group), lambda b: (0, b)),
            pl.BlockSpec((1, group), lambda b: (0, b)),
        ],
        out_specs=pl.BlockSpec((lines.shape[0], group), lambda b: (0, b)),
        out_shape=jax.ShapeDtypeStruct(lines.shape, jnp.bfloat16),
        name="order_kz",
    )(lines, rank)
    count = 2 * coils * rows_out
    each = 2 * coils * x_here
    sent = lax.all_to_all(
        ordered[:count].reshape(slab_total, each, blocks), "slab", 0, 0, tiled=True
    )
    spots = jnp.broadcast_to(ordered[count : count + 2][None], (slab_total, 2, blocks))
    spots = lax.all_to_all(spots, "slab", 0, 0, tiled=True).astype(jnp.int32)
    kz_all = spots[:, 0:1]
    ky_all = spots[:, 1:2]

    chunk = math.gcd(blocks, 256)
    span = 64
    width = math.gcd(blocks, 1024)
    per_row = blocks // width
    by_chunk = kz_all.reshape(slab_total * blocks // chunk, chunk)
    low = jnp.min(by_chunk, axis=1) // 8 * 8
    high = (jnp.max(by_chunk, axis=1) - low) // span + 1
    ytab, ztab = right_table(freq), left_table(depth)
    pairs = each // 2
    imaged = pl.pallas_call(
        functools.partial(add_kernel, chunk, span),
        grid_spec=pltpu.PrefetchScalarGridSpec(
            num_scalar_prefetch=2,
            grid=(slab_total * per_row,),
            in_specs=[
                pl.BlockSpec((1, each, width), lambda i, a, b: (i // per_row, 0, i % per_row)),
                pl.BlockSpec((1, 1, width), lambda i, a, b: (i // per_row, 0, i % per_row)),
                pl.BlockSpec((1, 1, width), lambda i, a, b: (i // per_row, 0, i % per_row)),
                pl.BlockSpec(ytab.shape, lambda i, a, b: (0, 0)),
                pl.BlockSpec(ztab.shape, lambda i, a, b: (0, 0)),
            ],
            out_specs=pl.BlockSpec((pairs, depth, 2 * freq), lambda i, a, b: (0, 0, 0)),
            scratch_shapes=[pltpu.VMEM((each, depth + span, freq), jnp.float32)],
        ),
        out_shape=jax.ShapeDtypeStruct((pairs, depth, 2 * freq), jnp.bfloat16),
        name="add_yz",
    )(low, high, sent, kz_all, ky_all, ytab, ztab)

    split = imaged.reshape(pairs, slab_total, planes, 2 * freq)
    split = lax.all_to_all(jnp.swapaxes(split, 0, 1), "slab", 0, 0, tiled=True)
    split = split.reshape(slab_total, coils, x_here, planes, 2 * freq)
    split = jnp.transpose(split, (0, 2, 1, 3, 4)).reshape(
        coil_total, rows_out // coil_total, coils, planes, 2 * freq
    )
    split = lax.all_to_all(split, "coil", 0, 0, tiled=True)
    mine = jnp.transpose(split, (0, 2, 3, 1, 4)).reshape(sensitivity.shape).astype(jnp.float32)
    maps = sensitivity.astype(jnp.float32)
    map_re, map_im = maps[..., :freq], maps[..., freq:]
    img_re, img_im = mine[..., :freq], mine[..., freq:]
    real_part = jnp.sum(map_re * img_re + map_im * img_im, axis=0)
    imag_part = jnp.sum(map_re * img_im - map_im * img_re, axis=0)
    return jnp.concatenate([real_part, imag_part], axis=-1)


def solution(mesh):
    return jax.shard_map(
        per_device,
        mesh=mesh,
        in_specs=(
            P("coil", "slab", None),
            P("slab", None),
            P("slab"),
            P("slab"),
            P("slab", None),
            P(None, "slab", "coil", None),
        ),
        out_specs=P("slab", "coil", None),
        check_vma=False,
    )
```

```python
import functools
import math

import jax
import jax.numpy as jnp
from jax import lax
from jax.experimental import pallas as pl
from jax.experimental.pallas import tpu as pltpu
from jax.sharding import PartitionSpec as P

KX = 256
CELLS = 64
NT = (((1,), (1,)), ((), ()))


def twiddle(first, second, length):
    phase = (first * second % length).astype(jnp.float32) * (2.0 * math.pi / length)
    scale = 1.0 / math.sqrt(length)
    return (jnp.cos(phase) * scale, jnp.sin(phase) * scale)


def ints(count):
    return jnp.arange(count, dtype=jnp.int32)


def across_table(coils, rows_out, x_here):
    x0 = (KX - rows_out) // 2
    cosine, sine = twiddle(x0 + ints(rows_out)[:, None], ints(CELLS)[None, :], KX)
    upper = jnp.stack([cosine, -sine], axis=1)
    lower = jnp.stack([sine, cosine], axis=1)
    eye = jnp.eye(coils, dtype=jnp.float32)
    tables = []
    for one in (jnp.stack([upper, lower], axis=1), jnp.stack([-lower, upper], axis=1)):
        one = one.reshape(rows_out // x_here, 1, x_here, 2, 1, 2, CELLS)
        one = one * eye[None, :, None, None, :, None, None]
        tables.append(one.reshape(2 * coils * rows_out, 2 * coils * CELLS))
    return jnp.concatenate(tables, axis=0).astype(jnp.bfloat16)


def right_table(length):
    cosine, sine = twiddle(ints(length)[:, None], ints(length)[None, :], length)
    upper = jnp.concatenate([cosine, sine], axis=1)
    lower = jnp.concatenate([-sine, cosine], axis=1)
    return jnp.concatenate([upper, lower], axis=0).astype(jnp.bfloat16)


def left_table(length):
    cosine, sine = twiddle(ints(length)[:, None], ints(length)[None, :], length)
    upper = jnp.concatenate([cosine, -sine], axis=1)
    lower = jnp.concatenate([sine, cosine], axis=1)
    return jnp.concatenate([upper, lower], axis=0).astype(jnp.bfloat16)


def grid_kernel(coils, pos_ref, val_ref, seg_ref, x_ref, tab_ref, out_ref, wide, where):
    lanes = wide.shape[2]
    rows = out_ref.shape[0]
    mid = (lax.broadcasted_iota(jnp.int32, (CELLS, lanes), 0).astype(jnp.float32) + 0.5) * 0.4

    @pl.loop(0, pos_ref.shape[1] // lanes)
    def _(at):
        cut = pl.ds(pl.multiple_of(at * lanes, lanes), lanes)
        for c in range(coils):
            wide[c] = val_ref[c, cut, :].astype(jnp.float32).T
        where[...] = pos_ref[:, cut]

        def step(i, sums):
            offset = where[pl.ds(i, 1), :] - mid
            bump = jnp.maximum(1.0 - offset * offset, 0.0)
            weight = (bump * bump).astype(jnp.bfloat16).astype(jnp.float32)
            return tuple(
                sums[n] + weight * wide[n // 2, pl.ds(n % 2 * CELLS + i, 1), :]
                for n in range(2 * coils)
            )

        zero = jnp.zeros((CELLS, lanes), jnp.float32)
        sums = lax.fori_loop(0, CELLS, step, (zero,) * (2 * coils), unroll=4)
        turn = (x_ref[...] * seg_ref[:, cut]) & 3
        cells = jnp.concatenate([part.astype(jnp.bfloat16) for part in sums], axis=0)
        moved = jnp.dot(tab_ref[...], cells, preferred_element_type=jnp.float32)
        turned = jnp.where((turn & 1) == 0, moved[:rows], moved[rows:])
        out_ref[:, cut] = jnp.where(turn >= 2, -turned, turned).astype(jnp.bfloat16)


def sort_kernel(vals_ref, spot_ref, rank_ref, out_ref, spot_out_ref):
    rows, group = vals_ref.shape
    tile = math.gcd(256, group)
    slot = lax.broadcasted_iota(jnp.int32, (tile, group), 0)
    vals = jnp.concatenate([vals_ref[...], spot_ref[...]], axis=0)

    @pl.loop(0, group // tile)
    def _(at):
        start = pl.multiple_of(at * tile, tile)
        hot = jnp.where(slot == (rank_ref[...] - start), 1.0, 0.0).astype(jnp.bfloat16)
        moved = lax.dot_general(vals, hot, NT, preferred_element_type=jnp.float32)
        moved = moved.astype(jnp.bfloat16)
        out_ref[:, pl.ds(start, tile)] = moved[:rows]
        spot_out_ref[:, pl.ds(start, tile)] = moved[rows:]


def add_kernel(
    chunk, span, lo_ref, more_ref, vals_ref, kz_ref, ky_ref, ytab_ref, ztab_ref, out_ref, total
):
    step = pl.program_id(0)
    rows = vals_ref.shape[1]
    width = vals_ref.shape[2]
    depth, freq = out_ref.shape[1], total.shape[2]
    parts = width // chunk
    spot = lax.broadcasted_iota(jnp.int32, (freq, chunk), 0)
    plane = lax.broadcasted_iota(jnp.int32, (span, chunk), 0)

    @pl.when(step == 0)
    def _():
        total[...] = jnp.zeros_like(total)

    def add(part, start):
        cut = slice(part * chunk, (part + 1) * chunk)
        hot = jnp.where(spot == ky_ref[0, :, cut], 1.0, 0.0).astype(jnp.bfloat16)
        mine = jnp.where(plane == (kz_ref[0, :, cut] - start), 1.0, 0.0).astype(jnp.bfloat16)
        left = []
        for v in range(rows):
            row = vals_ref[0, v : v + 1, cut].astype(jnp.float32)
            row = jnp.broadcast_to(row, (16, chunk)).astype(jnp.bfloat16)
            left.append(mine * jnp.concatenate([row] * (span // 16), axis=0))
        left = jnp.concatenate(left, axis=0)
        moved = lax.dot_general(left, hot, NT, preferred_element_type=jnp.float32)
        for v in range(rows):
            total[v, pl.ds(start, span), :] += moved[v * span : (v + 1) * span]

    for part in range(parts):
        add(part, pl.multiple_of(lo_ref[step * parts + part], 8))

    for part in range(parts):
        first = lo_ref[step * parts + part]

        def again(at, carry):
            add(part, pl.multiple_of(first + at * span, 8))
            return carry

        lax.fori_loop(1, more_ref[step * parts + part], again, 0)

    @pl.when(step == pl.num_programs(0) - 1)
    def _():
        pairs = rows // 2
        for pair in range(pairs):
            both = jnp.concatenate(
                [total[2 * pair, :depth, :], total[2 * pair + 1, :depth, :]], axis=1
            )
            planes = jnp.dot(
                both.astype(jnp.bfloat16), ytab_ref[...], preferred_element_type=jnp.float32
            ).astype(jnp.bfloat16)
            planes = jnp.concatenate([planes[:, :freq], planes[:, freq:]], axis=0)
            image = jnp.dot(ztab_ref[...], planes, preferred_element_type=jnp.float32)
            out_ref[pair, :, :freq] = image[:depth].astype(jnp.bfloat16)
            out_ref[pair, :, freq:] = image[depth:].astype(jnp.bfloat16)


def whole(memory=pltpu.VMEM):
    return pl.BlockSpec(memory_space=memory)


def per_device(samples, sample_pos, block_count, grid_block, block_slab, sensitivity):
    slab_total = lax.axis_size("slab")
    coil_total = lax.axis_size("coil")
    coils = samples.shape[0]
    blocks = samples.shape[1]
    planes = sensitivity.shape[1]
    rows_out = sensitivity.shape[2] * coil_total
    depth = planes * slab_total
    freq = sensitivity.shape[3] // 2
    x_here = rows_out // slab_total
    segments = KX // CELLS

    live = ints(CELLS)[:, None] < block_count[None, :]
    pos = jnp.where(live, sample_pos.T.astype(jnp.float32), 1.0e4) * 0.4
    seg = (grid_block % segments)[None, :]
    kz = block_slab[:, 0] * planes + grid_block // (segments * freq)
    ky = grid_block // segments % freq

    tile = math.gcd(blocks, 1024)
    lanes = math.gcd(tile, 128)
    count = 2 * coils * rows_out
    table = across_table(coils, rows_out, x_here)
    x_at = (ints(count) // (2 * coils * x_here)) * x_here + ints(count) // 2 % x_here
    x_at = jnp.broadcast_to((x_at + (KX - rows_out) // 2)[:, None], (count, lanes))
    lines = pl.pallas_call(
        functools.partial(grid_kernel, coils),
        grid=(blocks // tile,),
        in_specs=[
            pl.BlockSpec((CELLS, tile), lambda b: (0, b)),
            pl.BlockSpec((coils, tile, 2 * CELLS), lambda b: (0, b, 0)),
            pl.BlockSpec((1, tile), lambda b: (0, b)),
            pl.BlockSpec(x_at.shape, lambda b: (0, 0)),
            pl.BlockSpec(table.shape, lambda b: (0, 0)),
        ],
        out_specs=pl.BlockSpec((count, tile), lambda b: (0, b)),
        out_shape=jax.ShapeDtypeStruct((count, blocks), jnp.bfloat16),
        scratch_shapes=[
            pltpu.VMEM((coils, 2 * CELLS, lanes), jnp.float32),
            pltpu.VMEM((CELLS, lanes), jnp.float32),
        ],
        name="grid_x",
    )(pos, samples, seg, x_at, table)

    group = math.gcd(blocks, 2048)
    groups = blocks // group
    key = (kz * group + ints(blocks) % group).reshape(groups, group)
    rank = jnp.sum((key[:, :, None] < key[:, None, :]).astype(jnp.int32), axis=1)
    rank = rank.reshape(1, blocks)
    spots = jnp.pad(jnp.stack([kz, ky]).astype(jnp.bfloat16), ((0, 14), (0, 0)))
    ordered, spots = pl.pallas_call(
        sort_kernel,
        grid=(groups,),
        in_specs=[
            pl.BlockSpec((count, group), lambda b: (0, b)),
            pl.BlockSpec((16, group), lambda b: (0, b)),
            pl.BlockSpec((1, group), lambda b: (0, b)),
        ],
        out_specs=[
            pl.BlockSpec((count, group), lambda b: (0, b)),
            pl.BlockSpec((16, group), lambda b: (0, b)),
        ],
        out_shape=[
            jax.ShapeDtypeStruct((count, blocks), jnp.bfloat16),
            jax.ShapeDtypeStruct((16, blocks), jnp.bfloat16),
        ],
        name="order_kz",
    )(lines, spots, rank)
    each = 2 * coils * x_here
    sent = lax.all_to_all(
        ordered.reshape(slab_total, each, blocks), "slab", 0, 0, tiled=True
    )
    spots = jnp.broadcast_to(spots[:2][None], (slab_total, 2, blocks))
    spots = lax.all_to_all(spots, "slab", 0, 0, tiled=True).astype(jnp.int32)
    kz_all = spots[:, 0:1]
    ky_all = spots[:, 1:2]

    chunk = math.gcd(blocks, 256)
    span = 64
    width = math.gcd(blocks, 1024)
    per_row = blocks // width
    by_chunk = kz_all.reshape(slab_total * blocks // chunk, chunk)
    low = jnp.min(by_chunk, axis=1) // 8 * 8
    high = (jnp.max(by_chunk, axis=1) - low) // span + 1
    ytab, ztab = right_table(freq), left_table(depth)
    pairs = each // 2
    imaged = pl.pallas_call(
        functools.partial(add_kernel, chunk, span),
        grid_spec=pltpu.PrefetchScalarGridSpec(
            num_scalar_prefetch=2,
            grid=(slab_total * per_row,),
            in_specs=[
                pl.BlockSpec((1, each, width), lambda i, a, b: (i // per_row, 0, i % per_row)),
                pl.BlockSpec((1, 1, width), lambda i, a, b: (i // per_row, 0, i % per_row)),
                pl.BlockSpec((1, 1, width), lambda i, a, b: (i // per_row, 0, i % per_row)),
                pl.BlockSpec(ytab.shape, lambda i, a, b: (0, 0)),
                pl.BlockSpec(ztab.shape, lambda i, a, b: (0, 0)),
            ],
            out_specs=pl.BlockSpec((pairs, depth, 2 * freq), lambda i, a, b: (0, 0, 0)),
            scratch_shapes=[pltpu.VMEM((each, depth + span, freq), jnp.float32)],
        ),
        out_shape=jax.ShapeDtypeStruct((pairs, depth, 2 * freq), jnp.bfloat16),
        name="add_yz",
    )(low, high, sent, kz_all, ky_all, ytab, ztab)

    split = imaged.reshape(pairs, slab_total, planes, 2 * freq)
    split = lax.all_to_all(jnp.swapaxes(split, 0, 1), "slab", 0, 0, tiled=True)
    split = split.reshape(slab_total, coils, x_here, planes, 2 * freq)
    split = jnp.transpose(split, (0, 2, 1, 3, 4)).reshape(
        coil_total, rows_out // coil_total, coils, planes, 2 * freq
    )
    split = lax.all_to_all(split, "coil", 0, 0, tiled=True)
    mine = jnp.transpose(split, (0, 2, 3, 1, 4)).reshape(sensitivity.shape).astype(jnp.float32)
    maps = sensitivity.astype(jnp.float32)
    map_re, map_im = maps[..., :freq], maps[..., freq:]
    img_re, img_im = mine[..., :freq], mine[..., freq:]
    real_part = jnp.sum(map_re * img_re + map_im * img_im, axis=0)
    imag_part = jnp.sum(map_re * img_im - map_im * img_re, axis=0)
    return jnp.concatenate([real_part, imag_part], axis=-1)


def solution(mesh):
    return jax.shard_map(
        per_device,
        mesh=mesh,
        in_specs=(
            P("coil", "slab", None),
            P("slab", None),
            P("slab"),
            P("slab"),
            P("slab", None),
            P(None, "slab", "coil", None),
        ),
        out_specs=P("slab", "coil", None),
        check_vma=False,
    )
```

```python
import functools
import math

import jax
import jax.numpy as jnp
from jax import lax
from jax.experimental import pallas as pl
from jax.experimental.pallas import tpu as pltpu
from jax.sharding import PartitionSpec as P

KX = 256
CELLS = 64
NT = (((1,), (1,)), ((), ()))


def twiddle(first, second, length):
    phase = (first * second % length).astype(jnp.float32) * (2.0 * math.pi / length)
    scale = 1.0 / math.sqrt(length)
    return (jnp.cos(phase) * scale, jnp.sin(phase) * scale)


def ints(count):
    return jnp.arange(count, dtype=jnp.int32)


def across_table(coils, rows_out, x_here):
    x0 = (KX - rows_out) // 2
    cosine, sine = twiddle(x0 + ints(rows_out)[:, None], ints(CELLS)[None, :], KX)
    upper = jnp.stack([cosine, -sine], axis=1)
    lower = jnp.stack([sine, cosine], axis=1)
    eye = jnp.eye(coils, dtype=jnp.float32)
    tables = []
    for one in (jnp.stack([upper, lower], axis=1), jnp.stack([-lower, upper], axis=1)):
        one = one.reshape(rows_out // x_here, 1, x_here, 2, 1, 2, CELLS)
        one = one * eye[None, :, None, None, :, None, None]
        tables.append(one.reshape(2 * coils * rows_out, 2 * coils * CELLS))
    return jnp.concatenate(tables, axis=0).astype(jnp.bfloat16)


def right_table(length):
    cosine, sine = twiddle(ints(length)[:, None], ints(length)[None, :], length)
    upper = jnp.concatenate([cosine, sine], axis=1)
    lower = jnp.concatenate([-sine, cosine], axis=1)
    return jnp.concatenate([upper, lower], axis=0).astype(jnp.bfloat16)


def left_table(length):
    cosine, sine = twiddle(ints(length)[:, None], ints(length)[None, :], length)
    upper = jnp.concatenate([cosine, -sine], axis=1)
    lower = jnp.concatenate([sine, cosine], axis=1)
    return jnp.concatenate([upper, lower], axis=0).astype(jnp.bfloat16)


def grid_kernel(coils, pos_ref, val_ref, seg_ref, x_ref, tab_ref, out_ref, wide, where):
    lanes = wide.shape[2]
    rows = out_ref.shape[0]
    mid = (lax.broadcasted_iota(jnp.int32, (CELLS, lanes), 0).astype(jnp.float32) + 0.5) * 0.4

    @pl.loop(0, pos_ref.shape[1] // lanes)
    def _(at):
        cut = pl.ds(pl.multiple_of(at * lanes, lanes), lanes)
        for c in range(coils):
            wide[c] = val_ref[c, cut, :].astype(jnp.float32).T
        where[...] = pos_ref[:, cut]

        def step(i, sums):
            offset = where[pl.ds(i, 1), :] - mid
            bump = jnp.maximum(1.0 - offset * offset, 0.0)
            weight = (bump * bump).astype(jnp.bfloat16).astype(jnp.float32)
            return tuple(
                sums[n] + weight * wide[n // 2, pl.ds(n % 2 * CELLS + i, 1), :]
                for n in range(2 * coils)
            )

        zero = jnp.zeros((CELLS, lanes), jnp.float32)
        sums = lax.fori_loop(0, CELLS, step, (zero,) * (2 * coils), unroll=4)
        turn = (x_ref[...] * seg_ref[:, cut]) & 3
        cells = jnp.concatenate([part.astype(jnp.bfloat16) for part in sums], axis=0)
        moved = jnp.dot(tab_ref[...], cells, preferred_element_type=jnp.float32)
        turned = jnp.where((turn & 1) == 0, moved[:rows], moved[rows:])
        out_ref[:, cut] = jnp.where(turn >= 2, -turned, turned).astype(jnp.bfloat16)


def sort_kernel(vals_ref, spot_ref, kz_ref, out_ref, spot_out_ref, before, rank):
    rows, group = vals_ref.shape
    depth = before.shape[0]
    piece = math.gcd(128, group)
    pieces = group // piece
    level = lax.broadcasted_iota(jnp.int32, (depth, piece), 0)
    src = lax.broadcasted_iota(jnp.int32, (piece, 2 * piece), 0)
    dst = lax.broadcasted_iota(jnp.int32, (piece, 2 * piece), 1)
    steps = jnp.where((src < dst) | (dst >= piece), 1.0, 0.0).astype(jnp.bfloat16)
    seen = jnp.zeros((depth, piece), jnp.float32)
    for at in range(pieces):
        cut = slice(at * piece, (at + 1) * piece)
        hot = jnp.where(level == kz_ref[:, cut], 1.0, 0.0)
        counts = jnp.dot(hot.astype(jnp.bfloat16), steps, preferred_element_type=jnp.float32)
        before[:, cut] = seen + counts[:, :piece]
        seen = seen + counts[:, piece:]
    high = jnp.floor(seen * (1.0 / 256.0))
    low = seen - 256.0 * high
    here = lax.broadcasted_iota(jnp.int32, (depth, depth), 0)
    under = lax.broadcasted_iota(jnp.int32, (depth, depth), 1)
    lower = jnp.where(under < here, 1.0, 0.0).astype(jnp.bfloat16)
    first = 256.0 * jnp.dot(lower, high.astype(jnp.bfloat16), preferred_element_type=jnp.float32)
    first = first + jnp.dot(lower, low.astype(jnp.bfloat16), preferred_element_type=jnp.float32)
    for at in range(pieces):
        cut = slice(at * piece, (at + 1) * piece)
        found = jnp.where(level == kz_ref[:, cut], before[:, cut] + first, 0.0)
        rank[:, cut] = jnp.sum(found, axis=0, keepdims=True).astype(jnp.int32)

    tile = math.gcd(256, group)
    slot = lax.broadcasted_iota(jnp.int32, (tile, group), 0)
    vals = jnp.concatenate([vals_ref[...], spot_ref[...]], axis=0)

    @pl.loop(0, group // tile)
    def _(at):
        start = pl.multiple_of(at * tile, tile)
        hot = jnp.where(slot == (rank[...] - start), 1.0, 0.0).astype(jnp.bfloat16)
        moved = lax.dot_general(vals, hot, NT, preferred_element_type=jnp.float32)
        moved = moved.astype(jnp.bfloat16)
        out_ref[:, pl.ds(start, tile)] = moved[:rows]
        spot_out_ref[:, pl.ds(start, tile)] = moved[rows:]


def add_kernel(
    chunk, span, lo_ref, more_ref, vals_ref, kz_ref, ky_ref, ytab_ref, ztab_ref, out_ref, total
):
    step = pl.program_id(0)
    rows = vals_ref.shape[1]
    width = vals_ref.shape[2]
    depth, freq = out_ref.shape[1], total.shape[2]
    parts = width // chunk
    spot = lax.broadcasted_iota(jnp.int32, (freq, chunk), 0)
    plane = lax.broadcasted_iota(jnp.int32, (span, chunk), 0)

    @pl.when(step == 0)
    def _():
        total[...] = jnp.zeros_like(total)

    def add(part, start):
        cut = slice(part * chunk, (part + 1) * chunk)
        hot = jnp.where(spot == ky_ref[0, :, cut], 1.0, 0.0).astype(jnp.bfloat16)
        mine = jnp.where(plane == (kz_ref[0, :, cut] - start), 1.0, 0.0).astype(jnp.bfloat16)
        left = []
        for v in range(rows):
            row = vals_ref[0, v : v + 1, cut].astype(jnp.float32)
            row = jnp.broadcast_to(row, (16, chunk)).astype(jnp.bfloat16)
            left.append(mine * jnp.concatenate([row] * (span // 16), axis=0))
        left = jnp.concatenate(left, axis=0)
        moved = lax.dot_general(left, hot, NT, preferred_element_type=jnp.float32)
        for v in range(rows):
            total[v, pl.ds(start, span), :] += moved[v * span : (v + 1) * span]

    for part in range(parts):
        add(part, pl.multiple_of(lo_ref[step * parts + part], 8))

    for part in range(parts):
        first = lo_ref[step * parts + part]

        def again(at, carry):
            add(part, pl.multiple_of(first + at * span, 8))
            return carry

        lax.fori_loop(1, more_ref[step * parts + part], again, 0)

    @pl.when(step == pl.num_programs(0) - 1)
    def _():
        pairs = rows // 2
        for pair in range(pairs):
            both = jnp.concatenate(
                [total[2 * pair, :depth, :], total[2 * pair + 1, :depth, :]], axis=1
            )
            planes = jnp.dot(
                both.astype(jnp.bfloat16), ytab_ref[...], preferred_element_type=jnp.float32
            ).astype(jnp.bfloat16)
            planes = jnp.concatenate([planes[:, :freq], planes[:, freq:]], axis=0)
            image = jnp.dot(ztab_ref[...], planes, preferred_element_type=jnp.float32)
            out_ref[pair, :, :freq] = image[:depth].astype(jnp.bfloat16)
            out_ref[pair, :, freq:] = image[depth:].astype(jnp.bfloat16)


def whole(memory=pltpu.VMEM):
    return pl.BlockSpec(memory_space=memory)


def per_device(samples, sample_pos, block_count, grid_block, block_slab, sensitivity):
    slab_total = lax.axis_size("slab")
    coil_total = lax.axis_size("coil")
    coils = samples.shape[0]
    blocks = samples.shape[1]
    planes = sensitivity.shape[1]
    rows_out = sensitivity.shape[2] * coil_total
    depth = planes * slab_total
    freq = sensitivity.shape[3] // 2
    x_here = rows_out // slab_total
    segments = KX // CELLS

    live = ints(CELLS)[:, None] < block_count[None, :]
    pos = jnp.where(live, sample_pos.T.astype(jnp.float32), 1.0e4) * 0.4
    seg = (grid_block % segments)[None, :]
    kz = block_slab[:, 0] * planes + grid_block // (segments * freq)
    ky = grid_block // segments % freq

    tile = math.gcd(blocks, 1024)
    lanes = math.gcd(tile, 128)
    count = 2 * coils * rows_out
    table = across_table(coils, rows_out, x_here)
    x_at = (ints(count) // (2 * coils * x_here)) * x_here + ints(count) // 2 % x_here
    x_at = jnp.broadcast_to((x_at + (KX - rows_out) // 2)[:, None], (count, lanes))
    lines = pl.pallas_call(
        functools.partial(grid_kernel, coils),
        grid=(blocks // tile,),
        in_specs=[
            pl.BlockSpec((CELLS, tile), lambda b: (0, b)),
            pl.BlockSpec((coils, tile, 2 * CELLS), lambda b: (0, b, 0)),
            pl.BlockSpec((1, tile), lambda b: (0, b)),
            pl.BlockSpec(x_at.shape, lambda b: (0, 0)),
            pl.BlockSpec(table.shape, lambda b: (0, 0)),
        ],
        out_specs=pl.BlockSpec((count, tile), lambda b: (0, b)),
        out_shape=jax.ShapeDtypeStruct((count, blocks), jnp.bfloat16),
        scratch_shapes=[
            pltpu.VMEM((coils, 2 * CELLS, lanes), jnp.float32),
            pltpu.VMEM((CELLS, lanes), jnp.float32),
        ],
        name="grid_x",
    )(pos, samples, seg, x_at, table)

    group = math.gcd(blocks, 2048)
    groups = blocks // group
    spots = jnp.pad(jnp.stack([kz, ky]).astype(jnp.bfloat16), ((0, 14), (0, 0)))
    ordered, spots = pl.pallas_call(
        sort_kernel,
        grid=(groups,),
        in_specs=[
            pl.BlockSpec((count, group), lambda b: (0, b)),
            pl.BlockSpec((16, group), lambda b: (0, b)),
            pl.BlockSpec((1, group), lambda b: (0, b)),
        ],
        out_specs=[
            pl.BlockSpec((count, group), lambda b: (0, b)),
            pl.BlockSpec((16, group), lambda b: (0, b)),
        ],
        out_shape=[
            jax.ShapeDtypeStruct((count, blocks), jnp.bfloat16),
            jax.ShapeDtypeStruct((16, blocks), jnp.bfloat16),
        ],
        scratch_shapes=[
            pltpu.VMEM((depth, group), jnp.float32),
            pltpu.VMEM((1, group), jnp.int32),
        ],
        name="order_kz",
    )(lines, spots, kz[None, :])
    each = 2 * coils * x_here
    tail = jnp.broadcast_to(spots[:2].reshape(1, each, -1), (slab_total, each, 2 * blocks // each))
    sent = lax.all_to_all(
        jnp.concatenate([ordered.reshape(slab_total, each, blocks), tail], axis=2),
        "slab",
        0,
        0,
        tiled=True,
    )
    spots = sent[:, :, blocks:].reshape(slab_total, 2, blocks).astype(jnp.int32)
    kz_all = spots[:, 0:1]
    ky_all = spots[:, 1:2]

    chunk = math.gcd(blocks, 256)
    span = 64
    width = math.gcd(blocks, 1024)
    per_row = blocks // width
    by_chunk = kz_all.reshape(slab_total * blocks // chunk, chunk)
    low = jnp.min(by_chunk, axis=1) // 8 * 8
    high = (jnp.max(by_chunk, axis=1) - low) // span + 1
    ytab, ztab = right_table(freq), left_table(depth)
    pairs = each // 2
    imaged = pl.pallas_call(
        functools.partial(add_kernel, chunk, span),
        grid_spec=pltpu.PrefetchScalarGridSpec(
            num_scalar_prefetch=2,
            grid=(slab_total * per_row,),
            in_specs=[
                pl.BlockSpec((1, each, width), lambda i, a, b: (i // per_row, 0, i % per_row)),
                pl.BlockSpec((1, 1, width), lambda i, a, b: (i // per_row, 0, i % per_row)),
                pl.BlockSpec((1, 1, width), lambda i, a, b: (i // per_row, 0, i % per_row)),
                pl.BlockSpec(ytab.shape, lambda i, a, b: (0, 0)),
                pl.BlockSpec(ztab.shape, lambda i, a, b: (0, 0)),
            ],
            out_specs=pl.BlockSpec((pairs, depth, 2 * freq), lambda i, a, b: (0, 0, 0)),
            scratch_shapes=[pltpu.VMEM((each, depth + span, freq), jnp.float32)],
        ),
        out_shape=jax.ShapeDtypeStruct((pairs, depth, 2 * freq), jnp.bfloat16),
        name="add_yz",
    )(low, high, sent, kz_all, ky_all, ytab, ztab)

    split = imaged.reshape(pairs, slab_total, planes, 2 * freq)
    split = lax.all_to_all(jnp.swapaxes(split, 0, 1), "slab", 0, 0, tiled=True)
    split = split.reshape(slab_total, coils, x_here, planes, 2 * freq)
    split = jnp.transpose(split, (0, 2, 1, 3, 4)).reshape(
        coil_total, rows_out // coil_total, coils, planes, 2 * freq
    )
    split = lax.all_to_all(split, "coil", 0, 0, tiled=True)
    mine = jnp.transpose(split, (0, 2, 3, 1, 4)).reshape(sensitivity.shape).astype(jnp.float32)
    maps = sensitivity.astype(jnp.float32)
    map_re, map_im = maps[..., :freq], maps[..., freq:]
    img_re, img_im = mine[..., :freq], mine[..., freq:]
    real_part = jnp.sum(map_re * img_re + map_im * img_im, axis=0)
    imag_part = jnp.sum(map_re * img_im - map_im * img_re, axis=0)
    return jnp.concatenate([real_part, imag_part], axis=-1)


def solution(mesh):
    return jax.shard_map(
        per_device,
        mesh=mesh,
        in_specs=(
            P("coil", "slab", None),
            P("slab", None),
            P("slab"),
            P("slab"),
            P("slab", None),
            P(None, "slab", "coil", None),
        ),
        out_specs=P("slab", "coil", None),
        check_vma=False,
    )
```

```python
import functools
import math

import jax
import jax.numpy as jnp
from jax import lax
from jax.experimental import pallas as pl
from jax.experimental.pallas import tpu as pltpu
from jax.sharding import PartitionSpec as P

KX = 256
CELLS = 64
NT = (((1,), (1,)), ((), ()))


def twiddle(first, second, length):
    phase = (first * second % length).astype(jnp.float32) * (2.0 * math.pi / length)
    scale = 1.0 / math.sqrt(length)
    return (jnp.cos(phase) * scale, jnp.sin(phase) * scale)


def ints(count):
    return jnp.arange(count, dtype=jnp.int32)


def across_table(coils, rows_out, x_here):
    x0 = (KX - rows_out) // 2
    cosine, sine = twiddle(x0 + ints(rows_out)[:, None], ints(CELLS)[None, :], KX)
    upper = jnp.stack([cosine, -sine], axis=1)
    lower = jnp.stack([sine, cosine], axis=1)
    eye = jnp.eye(coils, dtype=jnp.float32)
    tables = []
    for one in (jnp.stack([upper, lower], axis=1), jnp.stack([-lower, upper], axis=1)):
        one = one.reshape(rows_out // x_here, 1, x_here, 2, 1, 2, CELLS)
        one = one * eye[None, :, None, None, :, None, None]
        tables.append(one.reshape(2 * coils * rows_out, 2 * coils * CELLS))
    return jnp.concatenate(tables, axis=0).astype(jnp.bfloat16)


def right_table(length):
    cosine, sine = twiddle(ints(length)[:, None], ints(length)[None, :], length)
    upper = jnp.concatenate([cosine, sine], axis=1)
    lower = jnp.concatenate([-sine, cosine], axis=1)
    return jnp.concatenate([upper, lower], axis=0).astype(jnp.bfloat16)


def left_table(length):
    cosine, sine = twiddle(ints(length)[:, None], ints(length)[None, :], length)
    upper = jnp.concatenate([cosine, -sine], axis=1)
    lower = jnp.concatenate([sine, cosine], axis=1)
    return jnp.concatenate([upper, lower], axis=0).astype(jnp.bfloat16)


def grid_kernel(coils, pos_ref, val_ref, seg_ref, x_ref, tab_ref, out_ref, wide, where):
    lanes = wide.shape[2]
    rows = out_ref.shape[0]
    mid = (lax.broadcasted_iota(jnp.int32, (CELLS, lanes), 0).astype(jnp.float32) + 0.5) * 0.4

    @pl.loop(0, pos_ref.shape[1] // lanes)
    def _(at):
        cut = pl.ds(pl.multiple_of(at * lanes, lanes), lanes)
        for c in range(coils):
            wide[c] = val_ref[c, cut, :].astype(jnp.float32).T
        where[...] = pos_ref[:, cut]

        def step(i, sums):
            offset = where[pl.ds(i, 1), :] - mid
            bump = jnp.maximum(1.0 - offset * offset, 0.0)
            weight = (bump * bump).astype(jnp.bfloat16).astype(jnp.float32)
            return tuple(
                sums[n] + weight * wide[n // 2, pl.ds(n % 2 * CELLS + i, 1), :]
                for n in range(2 * coils)
            )

        zero = jnp.zeros((CELLS, lanes), jnp.float32)
        sums = lax.fori_loop(0, CELLS, step, (zero,) * (2 * coils), unroll=16)
        turn = (x_ref[...] * seg_ref[:, cut]) & 3
        cells = jnp.concatenate([part.astype(jnp.bfloat16) for part in sums], axis=0)
        moved = jnp.dot(tab_ref[...], cells, preferred_element_type=jnp.float32)
        turned = jnp.where((turn & 1) == 0, moved[:rows], moved[rows:])
        out_ref[:, cut] = jnp.where(turn >= 2, -turned, turned).astype(jnp.bfloat16)


def sort_kernel(vals_ref, spot_ref, kz_ref, out_ref, spot_out_ref, before, rank):
    rows, group = vals_ref.shape
    depth = before.shape[0]
    piece = math.gcd(128, group)
    pieces = group // piece
    level = lax.broadcasted_iota(jnp.int32, (depth, piece), 0)
    src = lax.broadcasted_iota(jnp.int32, (piece, 2 * piece), 0)
    dst = lax.broadcasted_iota(jnp.int32, (piece, 2 * piece), 1)
    steps = jnp.where((src < dst) | (dst >= piece), 1.0, 0.0).astype(jnp.bfloat16)
    seen = jnp.zeros((depth, piece), jnp.float32)
    for at in range(pieces):
        cut = slice(at * piece, (at + 1) * piece)
        hot = jnp.where(level == kz_ref[:, cut], 1.0, 0.0)
        counts = jnp.dot(hot.astype(jnp.bfloat16), steps, preferred_element_type=jnp.float32)
        before[:, cut] = seen + counts[:, :piece]
        seen = seen + counts[:, piece:]
    high = jnp.floor(seen * (1.0 / 256.0))
    low = seen - 256.0 * high
    here = lax.broadcasted_iota(jnp.int32, (depth, depth), 0)
    under = lax.broadcasted_iota(jnp.int32, (depth, depth), 1)
    lower = jnp.where(under < here, 1.0, 0.0).astype(jnp.bfloat16)
    first = 256.0 * jnp.dot(lower, high.astype(jnp.bfloat16), preferred_element_type=jnp.float32)
    first = first + jnp.dot(lower, low.astype(jnp.bfloat16), preferred_element_type=jnp.float32)
    for at in range(pieces):
        cut = slice(at * piece, (at + 1) * piece)
        found = jnp.where(level == kz_ref[:, cut], before[:, cut] + first, 0.0)
        rank[:, cut] = jnp.sum(found, axis=0, keepdims=True).astype(jnp.int32)

    tile = math.gcd(256, group)
    slot = lax.broadcasted_iota(jnp.int32, (tile, group), 0)
    vals = jnp.concatenate([vals_ref[...], spot_ref[...]], axis=0)

    @pl.loop(0, group // tile)
    def _(at):
        start = pl.multiple_of(at * tile, tile)
        hot = jnp.where(slot == (rank[...] - start), 1.0, 0.0).astype(jnp.bfloat16)
        moved = lax.dot_general(vals, hot, NT, preferred_element_type=jnp.float32)
        moved = moved.astype(jnp.bfloat16)
        out_ref[:, pl.ds(start, tile)] = moved[:rows]
        spot_out_ref[:, pl.ds(start, tile)] = moved[rows:]


def add_kernel(
    chunk, span, lo_ref, more_ref, vals_ref, kz_ref, ky_ref, ytab_ref, ztab_ref, out_ref, total
):
    step = pl.program_id(0)
    rows = vals_ref.shape[1]
    width = vals_ref.shape[2]
    depth, freq = out_ref.shape[1], total.shape[2]
    parts = width // chunk
    spot = lax.broadcasted_iota(jnp.int32, (freq, chunk), 0)
    plane = lax.broadcasted_iota(jnp.int32, (span, chunk), 0)

    @pl.when(step == 0)
    def _():
        total[...] = jnp.zeros_like(total)

    def add(part, start):
        cut = slice(part * chunk, (part + 1) * chunk)
        hot = jnp.where(spot == ky_ref[0, :, cut], 1.0, 0.0).astype(jnp.bfloat16)
        mine = jnp.where(plane == (kz_ref[0, :, cut] - start), 1.0, 0.0).astype(jnp.bfloat16)
        left = []
        for v in range(rows):
            row = vals_ref[0, v : v + 1, cut].astype(jnp.float32)
            row = jnp.broadcast_to(row, (16, chunk)).astype(jnp.bfloat16)
            left.append(mine * jnp.concatenate([row] * (span // 16), axis=0))
        left = jnp.concatenate(left, axis=0)
        moved = lax.dot_general(left, hot, NT, preferred_element_type=jnp.float32)
        for v in range(rows):
            total[v, pl.ds(start, span), :] += moved[v * span : (v + 1) * span]

    for part in range(parts):
        add(part, pl.multiple_of(lo_ref[step * parts + part], 8))

    for part in range(parts):
        first = lo_ref[step * parts + part]

        def again(at, carry):
            add(part, pl.multiple_of(first + at * span, 8))
            return carry

        lax.fori_loop(1, more_ref[step * parts + part], again, 0)

    @pl.when(step == pl.num_programs(0) - 1)
    def _():
        pairs = rows // 2
        for pair in range(pairs):
            both = jnp.concatenate(
                [total[2 * pair, :depth, :], total[2 * pair + 1, :depth, :]], axis=1
            )
            planes = jnp.dot(
                both.astype(jnp.bfloat16), ytab_ref[...], preferred_element_type=jnp.float32
            ).astype(jnp.bfloat16)
            planes = jnp.concatenate([planes[:, :freq], planes[:, freq:]], axis=0)
            image = jnp.dot(ztab_ref[...], planes, preferred_element_type=jnp.float32)
            out_ref[pair, :, :freq] = image[:depth].astype(jnp.bfloat16)
            out_ref[pair, :, freq:] = image[depth:].astype(jnp.bfloat16)


def whole(memory=pltpu.VMEM):
    return pl.BlockSpec(memory_space=memory)


def per_device(samples, sample_pos, block_count, grid_block, block_slab, sensitivity):
    slab_total = lax.axis_size("slab")
    coil_total = lax.axis_size("coil")
    coils = samples.shape[0]
    blocks = samples.shape[1]
    planes = sensitivity.shape[1]
    rows_out = sensitivity.shape[2] * coil_total
    depth = planes * slab_total
    freq = sensitivity.shape[3] // 2
    x_here = rows_out // slab_total
    segments = KX // CELLS

    live = ints(CELLS)[:, None] < block_count[None, :]
    pos = jnp.where(live, sample_pos.T.astype(jnp.float32), 1.0e4) * 0.4
    seg = (grid_block % segments)[None, :]
    kz = block_slab[:, 0] * planes + grid_block // (segments * freq)
    ky = grid_block // segments % freq

    tile = math.gcd(blocks, 1024)
    lanes = math.gcd(tile, 128)
    count = 2 * coils * rows_out
    table = across_table(coils, rows_out, x_here)
    x_at = (ints(count) // (2 * coils * x_here)) * x_here + ints(count) // 2 % x_here
    x_at = jnp.broadcast_to((x_at + (KX - rows_out) // 2)[:, None], (count, lanes))
    lines = pl.pallas_call(
        functools.partial(grid_kernel, coils),
        grid=(blocks // tile,),
        in_specs=[
            pl.BlockSpec((CELLS, tile), lambda b: (0, b)),
            pl.BlockSpec((coils, tile, 2 * CELLS), lambda b: (0, b, 0)),
            pl.BlockSpec((1, tile), lambda b: (0, b)),
            pl.BlockSpec(x_at.shape, lambda b: (0, 0)),
            pl.BlockSpec(table.shape, lambda b: (0, 0)),
        ],
        out_specs=pl.BlockSpec((count, tile), lambda b: (0, b)),
        out_shape=jax.ShapeDtypeStruct((count, blocks), jnp.bfloat16),
        scratch_shapes=[
            pltpu.VMEM((coils, 2 * CELLS, lanes), jnp.float32),
            pltpu.VMEM((CELLS, lanes), jnp.float32),
        ],
        name="grid_x",
    )(pos, samples, seg, x_at, table)

    group = math.gcd(blocks, 2048)
    groups = blocks // group
    spots = jnp.pad(jnp.stack([kz, ky]).astype(jnp.bfloat16), ((0, 14), (0, 0)))
    ordered, spots = pl.pallas_call(
        sort_kernel,
        grid=(groups,),
        in_specs=[
            pl.BlockSpec((count, group), lambda b: (0, b)),
            pl.BlockSpec((16, group), lambda b: (0, b)),
            pl.BlockSpec((1, group), lambda b: (0, b)),
        ],
        out_specs=[
            pl.BlockSpec((count, group), lambda b: (0, b)),
            pl.BlockSpec((16, group), lambda b: (0, b)),
        ],
        out_shape=[
            jax.ShapeDtypeStruct((count, blocks), jnp.bfloat16),
            jax.ShapeDtypeStruct((16, blocks), jnp.bfloat16),
        ],
        scratch_shapes=[
            pltpu.VMEM((depth, group), jnp.float32),
            pltpu.VMEM((1, group), jnp.int32),
        ],
        name="order_kz",
    )(lines, spots, kz[None, :])
    each = 2 * coils * x_here
    tail = jnp.broadcast_to(spots[:2].reshape(1, each, -1), (slab_total, each, 2 * blocks // each))
    sent = lax.all_to_all(
        jnp.concatenate([ordered.reshape(slab_total, each, blocks), tail], axis=2),
        "slab",
        0,
        0,
        tiled=True,
    )
    spots = sent[:, :, blocks:].reshape(slab_total, 2, blocks).astype(jnp.int32)
    kz_all = spots[:, 0:1]
    ky_all = spots[:, 1:2]

    chunk = math.gcd(blocks, 256)
    span = 64
    width = math.gcd(blocks, 1024)
    per_row = blocks // width
    by_chunk = kz_all.reshape(slab_total * blocks // chunk, chunk)
    low = jnp.min(by_chunk, axis=1) // 8 * 8
    high = (jnp.max(by_chunk, axis=1) - low) // span + 1
    ytab, ztab = right_table(freq), left_table(depth)
    pairs = each // 2
    imaged = pl.pallas_call(
        functools.partial(add_kernel, chunk, span),
        grid_spec=pltpu.PrefetchScalarGridSpec(
            num_scalar_prefetch=2,
            grid=(slab_total * per_row,),
            in_specs=[
                pl.BlockSpec((1, each, width), lambda i, a, b: (i // per_row, 0, i % per_row)),
                pl.BlockSpec((1, 1, width), lambda i, a, b: (i // per_row, 0, i % per_row)),
                pl.BlockSpec((1, 1, width), lambda i, a, b: (i // per_row, 0, i % per_row)),
                pl.BlockSpec(ytab.shape, lambda i, a, b: (0, 0)),
                pl.BlockSpec(ztab.shape, lambda i, a, b: (0, 0)),
            ],
            out_specs=pl.BlockSpec((pairs, depth, 2 * freq), lambda i, a, b: (0, 0, 0)),
            scratch_shapes=[pltpu.VMEM((each, depth + span, freq), jnp.float32)],
        ),
        out_shape=jax.ShapeDtypeStruct((pairs, depth, 2 * freq), jnp.bfloat16),
        name="add_yz",
    )(low, high, sent, kz_all, ky_all, ytab, ztab)

    split = imaged.reshape(pairs, slab_total, planes, 2 * freq)
    split = lax.all_to_all(jnp.swapaxes(split, 0, 1), "slab", 0, 0, tiled=True)
    split = split.reshape(slab_total, coils, x_here, planes, 2 * freq)
    split = jnp.transpose(split, (0, 2, 1, 3, 4)).reshape(
        coil_total, rows_out // coil_total, coils, planes, 2 * freq
    )
    split = lax.all_to_all(split, "coil", 0, 0, tiled=True)
    mine = jnp.transpose(split, (0, 2, 3, 1, 4)).reshape(sensitivity.shape).astype(jnp.float32)
    maps = sensitivity.astype(jnp.float32)
    map_re, map_im = maps[..., :freq], maps[..., freq:]
    img_re, img_im = mine[..., :freq], mine[..., freq:]
    real_part = jnp.sum(map_re * img_re + map_im * img_im, axis=0)
    imag_part = jnp.sum(map_re * img_im - map_im * img_re, axis=0)
    return jnp.concatenate([real_part, imag_part], axis=-1)


def solution(mesh):
    return jax.shard_map(
        per_device,
        mesh=mesh,
        in_specs=(
            P("coil", "slab", None),
            P("slab", None),
            P("slab"),
            P("slab"),
            P("slab", None),
            P(None, "slab", "coil", None),
        ),
        out_specs=P("slab", "coil", None),
        check_vma=False,
    )
```
